32 devices in a mesh: req: 16 (over z, x, core), tp: 2 (over y).
Axes of the slice: x: 2, y: 2, z: 4, core: 2. Of those that a mesh axis runs over, the one named last changes fastest.
Arguments:
- state: bfloat16 [256, 2048], P('req'), may hold values from -3 to 3
- norm_gain: float32 [2048], replicated, may hold values from 0.25 to 4
- w_qkv: bfloat16 [2048, 2, 512], P(None, 'tp'), may hold values from -0.125 to 0.125
- w_out: bfloat16 [2, 256, 2048], P('tp'), may hold values from -0.25 to 0.25
- kv_cache: bfloat16 [2944, 2, 16, 256], P('req', 'tp')
- lengths: int32 [256], P('req'), may hold values from 32 to 1024, as said below
- page_table: int32 [256, 64], P('req'), may hold values from 0 to 183, as said below
- dest_slot: int32 [256], P('req'), may hold values from 0 to 255, as said below
Outputs:
- new_state: bfloat16 [256, 2048], P('req')
The draws below stay inside these ranges and needn't reach their ends.
Inputs may be any that keep to these rules, and one draw needn't show every extreme that they name: `lengths`: each device of req holds at most one request with more than 128 cached tokens; all others have 32 to 128; in every draw some request has exactly 1024. `page_table`: entry j of row r, for j below ceil(lengths[r] / 16), is the page (numbered within the home device r // 16) holding tokens j * 16 to (j + 1) * 16 - 1 of request r; no page serves two such entries; the entries after those are 183. dest_slot is a permutation. The request in slot k of device i of req (index i * 16 + k) goes to slot k of device (i + o_k) mod (16), with offsets o_k the same for all devices; at most 2 requests of one device go to one device, and exactly 2 do for some pairs.
All inputs are finite; a program needn't handle non-finite values.
Results may differ from the reference program's by a relative error of at most 0.01.
Values may be sent and summed in bfloat16 or wider, within the bound.
A program may use at most 64 MiB of HBM per device.

```python
import math
import jax
import jax.numpy as jnp
from jax import lax

D = 2048
HD = 128
GROUP = 2
REQ_DEV = 16
PAGE = 16
SHORT_LO = 32
SHORT_HI = 128
LONG_MAX = 1024
KVH = 2
MAXP = 64
PAGES_DEV = 184
PAGES = 2944
REQS = 256


def request_layout(key):
    base_key = jax.random.fold_in(key, 11)
    keys = jax.random.split(base_key, 6)
    device_count = REQS // REQ_DEV
    short_len = jax.random.randint(keys[0], (device_count, REQ_DEV), SHORT_LO, SHORT_HI + 1)
    has_long = jax.random.randint(keys[1], (device_count,), 0, 2)
    forced = jax.random.randint(keys[2], (), 0, device_count)
    device_ids = jnp.arange(device_count)
    has_long = jnp.where(device_ids == forced, 1, has_long)
    long_len = LONG_MAX - jax.random.randint(keys[3], (device_count,), 0, LONG_MAX // 2)
    long_len = jnp.where(device_ids == forced, LONG_MAX, long_len)
    long_slot = jax.random.randint(keys[4], (device_count,), 0, REQ_DEV)
    is_long = (has_long[:, None] == 1) & (jnp.arange(REQ_DEV)[None, :] == long_slot[:, None])
    req_len = jnp.where(is_long, long_len[:, None], short_len).astype(jnp.int32)
    page_count = (req_len + PAGE - 1) // PAGE
    perm_keys = jax.random.split(keys[5], device_count)
    orders = jax.vmap(lambda one_key: jax.random.permutation(one_key, PAGES_DEV))(perm_keys)
    starts = jnp.cumsum(page_count, axis=1) - page_count
    index_grid = starts[:, :, None] + jnp.arange(MAXP)[None, None, :]
    valid = jnp.arange(MAXP)[None, None, :] < page_count[:, :, None]
    clipped = jnp.clip(index_grid, 0, PAGES_DEV - 1).reshape(device_count, REQ_DEV * MAXP)
    table = jnp.take_along_axis(orders, clipped, axis=1).reshape(device_count, REQ_DEV, MAXP)
    table = jnp.where(valid, table, PAGES_DEV - 1).astype(jnp.int32)
    return (req_len.reshape(REQS), table.reshape(REQS, MAXP))


def draw_lengths(key, part):
    return request_layout(key)[0]


def draw_page_table(key, part):
    return request_layout(key)[1]


def draw_dest_slot(key, part):
    device_count = REQS // REQ_DEV
    half_way = device_count // 2
    order = jax.random.permutation(jax.random.fold_in(key, 23), device_count - 1)
    order = jnp.where(order >= half_way, order + 1, order)
    paired = jnp.full((2,), half_way, dtype=order.dtype)
    offsets = jnp.concatenate([paired, order[:REQ_DEV - 2]])
    devices = jnp.arange(device_count)[:, None]
    target = (devices + offsets[None, :]) % device_count * REQ_DEV + jnp.arange(REQ_DEV)[None, :]
    return target.reshape(REQS).astype(jnp.int32)


def draw_kv_cache(key, part):
    keys = jax.random.split(jax.random.fold_in(key, 5), 1)
    shape = (PAGES, KVH, PAGE, 2 * HD)
    base = jax.random.normal(keys[0], shape, jnp.float32)
    return base.astype(jnp.bfloat16)


def block_scale(stream_key, extent, cuts, low, largest):
    level = 1.0
    for position, blocks in cuts:
        steps = jax.random.uniform(jax.random.fold_in(jax.random.fold_in(stream_key, 6), position), (blocks,), jnp.float32, low / len(cuts), largest / len(cuts))
        level = level * jnp.repeat(jnp.exp(steps), extent[position] // blocks).reshape((-1,) + (1,) * (len(extent) - 1 - position))
    return level


def gaussian(stream_key, shape, width, bound, cuts=(), kind=jnp.bfloat16):
    level = block_scale(stream_key, shape, cuts, -0.22, 0.18) if cuts else 1.0
    entries = jax.random.normal(stream_key, shape, jnp.float32) * width * level
    return jnp.minimum(jnp.maximum(entries, -bound), bound).astype(kind)


def setup_inputs(seed: int = 0) -> dict:
    splits = jax.random.split(jax.random.key(seed), 9)
    return {
        "state": gaussian(splits[0], (REQS, D), 0.5, 3.0, ((0, 16),)),
        "norm_gain": jnp.clip(jnp.exp(jax.random.uniform(splits[1], (D,), jnp.float32, math.log(0.25), math.log(4.0))), 0.25, 4.0),
        "w_qkv": gaussian(splits[2], (D, KVH, (GROUP + 2) * HD), D ** -0.5, 0.125, ((1, 2),)),
        "w_out": gaussian(splits[3], (KVH, GROUP * HD, D), (KVH * GROUP * HD) ** -0.5, 0.25, ((0, 2),)),
        "kv_cache": draw_kv_cache(jax.random.fold_in(splits[8], 71), 0),
        "lengths": draw_lengths(jax.random.fold_in(splits[8], 71), 0),
        "page_table": draw_page_table(jax.random.fold_in(splits[8], 71), 0),
        "dest_slot": draw_dest_slot(jax.random.fold_in(splits[8], 71), 0),
    }


def normalize(values, scale_gain):
    wide = values.astype(jnp.float32)
    factor = lax.rsqrt(lax.optimization_barrier(jnp.mean(wide * wide, axis=-1, keepdims=True)) + 1e-05)
    return (wide * factor * scale_gain).astype(jnp.bfloat16)

def rotate(values, positions):
    half_size = values.shape[-1] // 2
    freqs = jnp.exp(-jnp.log(1000000.0) * 2.0 * jnp.arange(half_size, dtype=jnp.float32) / (2 * half_size))
    angles = positions.astype(jnp.float32)[:, None, None] * freqs
    cosine = jnp.cos(angles)
    sine = jnp.sin(angles)
    first = values[..., :half_size]
    second = values[..., half_size:]
    return jnp.concatenate([first * cosine - second * sine, second * cosine + first * sine], axis=-1)

def reference(state, norm_gain, w_qkv, w_out, kv_cache, lengths, page_table, dest_slot):
    total_rows = state.shape[0]
    devices_req = total_rows // REQ_DEV
    normed = normalize(state, norm_gain)
    proj = jnp.einsum('rd,dgc->rgc', normed.astype(jnp.float32), w_qkv.astype(jnp.float32))
    query = rotate(proj[..., :GROUP * HD].reshape(total_rows, KVH * GROUP, HD), lengths)
    query = query.astype(jnp.bfloat16).reshape(total_rows, KVH, GROUP, HD)
    new_key = rotate(proj[..., GROUP * HD:(GROUP + 1) * HD], lengths).astype(jnp.bfloat16)
    new_value = proj[..., (GROUP + 1) * HD:].astype(jnp.bfloat16)
    scale = 1.0 / jnp.sqrt(jnp.float32(HD))

    def per_device(inputs):
        dev_query, dev_key, dev_value, dev_len, dev_table, dev_pool = inputs
        picked = dev_pool[dev_table]
        picked = jnp.transpose(picked, (0, 2, 1, 3, 4)).reshape(REQ_DEV, KVH, MAXP * PAGE, 2 * HD)
        scores = jnp.einsum('rgjc,rgtc->rgjt', dev_query.astype(jnp.float32), picked[..., :HD].astype(jnp.float32)) * scale
        live = jnp.arange(MAXP * PAGE, dtype=jnp.int32)[None, :] < dev_len[:, None]
        scores = jnp.where(live[:, None, None, :], scores, -jnp.inf)
        score_new = jnp.einsum('rgjc,rgc->rgj', dev_query.astype(jnp.float32), dev_key.astype(jnp.float32)) * scale
        row_top = jnp.maximum(lax.optimization_barrier(jnp.max(scores, axis=-1)), score_new)
        weights = jnp.exp(scores - row_top[..., None])
        weight_new = jnp.exp(score_new - row_top)
        total = lax.optimization_barrier(jnp.sum(weights, axis=-1)) + weight_new
        numer = jnp.einsum('rgjt,rgtc->rgjc', weights.astype(jnp.bfloat16).astype(jnp.float32), picked[..., HD:].astype(jnp.float32))
        numer = numer + weight_new.astype(jnp.bfloat16).astype(jnp.float32)[..., None] * dev_value.astype(jnp.float32)[:, :, None, :]
        return (numer / total[..., None]).astype(jnp.bfloat16).reshape(REQ_DEV, KVH, GROUP * HD)
    attn = lax.map(per_device, (query.reshape(devices_req, REQ_DEV, KVH, GROUP, HD), new_key.reshape(devices_req, REQ_DEV, KVH, HD), new_value.reshape(devices_req, REQ_DEV, KVH, HD), lengths.reshape(devices_req, REQ_DEV), page_table.reshape(devices_req, REQ_DEV, MAXP), kv_cache.reshape(devices_req, PAGES_DEV, KVH, PAGE, 2 * HD)))
    attn = attn.reshape(total_rows, KVH, GROUP * HD)
    output = jnp.einsum('rgc,gcd->rd', attn.astype(jnp.float32), w_out.astype(jnp.float32))
    mixed = (state.astype(jnp.float32) + output).astype(jnp.bfloat16)
    return jnp.zeros_like(mixed).at[dest_slot].set(mixed)
```

```python
import functools
import math

import jax
import jax.numpy as jnp
from jax import lax
from jax.experimental import pallas as pl
from jax.experimental.pallas import tpu as pltpu
from jax.sharding import PartitionSpec as P

MESH = pl.DeviceIdType.MESH
LANES = 128
F32 = jnp.float32
BF16 = jnp.bfloat16


def iota(shape, axis):
    return lax.broadcasted_iota(jnp.int32, shape, axis)


def to_column(row):
    size = row.shape[1]
    eye = iota((size, size), 0) == iota((size, size), 1)
    return jnp.sum(jnp.where(eye, jnp.broadcast_to(row, (size, size)), 0.0), axis=1, keepdims=True)


def kernel(
    n,
    tp,
    page,
    state_ref,
    gain_ref,
    wqkv_hbm,
    wout_hbm,
    pool_hbm,
    len_ref,
    table_ref,
    dest_ref,
    out_ref,
    wqkv,
    wout,
    pool,
    parts,
    arrived,
    outgoing,
    incoming,
    gathered,
    load_sem,
    part_send,
    part_recv,
    move_send,
    move_recv,
    gather_send,
    gather_recv,
):
    rows, width = state_ref.shape
    group = wout.shape[0] // LANES
    chunk = width // tp
    blocks = chunk // LANES
    tokens = pool.shape[0]
    page_count = tokens // page
    me = lax.axis_index("req")
    my_part = lax.axis_index("tp")

    steps = 4
    depth = width // steps
    loads = []
    for step in range(steps):
        span = pl.ds(step * depth, depth)
        loads.append(pltpu.make_async_copy(wqkv_hbm.at[span], wqkv.at[span], load_sem.at[step]))
    load_pool = pltpu.make_async_copy(pool_hbm, pool, load_sem.at[steps])
    load_wout = pltpu.make_async_copy(wout_hbm, wout, load_sem.at[steps + 1])
    for load in loads:
        load.start()
    load_pool.start()
    load_wout.start()

    barrier = pltpu.get_barrier_semaphore()

    def greet(shift, carry):
        pl.semaphore_signal(
            barrier,
            inc=1,
            device_id={"req": lax.rem(me + shift, n), "tp": my_part},
            device_id_type=MESH,
        )
        return carry

    lax.fori_loop(1, n, greet, 0)
    for shift in range(1, tp):
        pl.semaphore_signal(
            barrier,
            inc=1,
            device_id={"req": me, "tp": lax.rem(my_part + shift, tp)},
            device_id_type=MESH,
        )

    wide = state_ref[...].astype(F32)
    factor = lax.rsqrt(jnp.mean(wide * wide, axis=-1, keepdims=True) + 1e-05)
    normed = (wide * factor * gain_ref[...]).astype(BF16)

    length = to_column(len_ref[...].astype(F32))
    lane = iota((rows, LANES), 1)
    half = LANES // 2
    index = lax.rem(lane, half).astype(F32)
    freqs = jnp.exp(-math.log(1000000.0) * 2.0 * index / LANES)
    angles = length * freqs
    cosine = jnp.cos(angles)
    sine = jnp.where(lane < half, -jnp.sin(angles), jnp.sin(angles))

    used = jnp.floor((length + (page - 1)) / page).astype(jnp.int32)
    table = table_ref[...]
    table = jnp.where(iota(table.shape, 1) < used, table, -1)
    padded = pl.cdiv(page_count, LANES) * LANES
    page_id = iota((rows, padded), 1)
    live_count = jnp.zeros((rows, padded), F32)
    for entry in range(table.shape[1]):
        left = length - float(entry * page)
        live_count = jnp.where(page_id == table[:, entry : entry + 1], left, live_count)
    live_count = jnp.clip(live_count, 0.0, float(page))
    per_block = LANES // page
    shifted = []
    for block in range(tokens // LANES):
        first = block * per_block
        base = first // LANES * LANES
        piece = live_count[:, base : base + LANES]
        if first != base:
            piece = pltpu.roll(piece, LANES - (first - base), 1)
        shifted.append(piece)
    spread = (iota((LANES, LANES), 0) == iota((LANES, LANES), 1) // page).astype(BF16)
    live_tokens = jnp.dot(
        jnp.concatenate(shifted, axis=0).astype(BF16), spread, preferred_element_type=F32
    )

    shift_bits = rows.bit_length() - 1
    target_row = lax.shift_right_logical(dest_ref[...], shift_bits).astype(F32)
    target = to_column(target_row)
    same = jnp.broadcast_to(target, (rows, rows)) == jnp.broadcast_to(target_row, (rows, rows))
    earlier = iota((rows, rows), 1) < iota((rows, rows), 0)
    rank = jnp.sum(jnp.where(same & earlier, 1.0, 0.0), axis=1, keepdims=True)
    source = (2 * me).astype(F32) - target
    source = jnp.where(source < 0, source + n, source)
    source = jnp.where(source >= n, source - n, source)
    key_out = (target * 2 + rank).astype(jnp.int32)
    key_in = (source * 2 + rank).astype(jnp.int32)
    flat = rows * blocks
    total_rows = n * 2 * blocks
    picked = iota((rows, flat), 0) == lax.rem(iota((rows, flat), 1), rows)
    key_row = jnp.sum(jnp.where(picked, key_out, 0).astype(F32), axis=0, keepdims=True).astype(
        jnp.int32
    )
    row_id = iota((total_rows, flat), 0)
    col_id = iota((total_rows, flat), 1)
    pack = (
        (row_id // blocks == key_row) & (lax.rem(row_id, blocks) == col_id // rows)
    ).astype(BF16)
    key_col = jnp.concatenate([key_in] * blocks, axis=0)
    row_id = iota((flat, total_rows), 0)
    col_id = iota((flat, total_rows), 1)
    unpack = (
        (col_id // blocks == key_col) & (lax.rem(col_id, blocks) == row_id // rows)
    ).astype(BF16)

    proj = None
    for step in range(steps):
        loads[step].wait()
        span = slice(step * depth, (step + 1) * depth)
        term = jnp.dot(normed[:, span], wqkv[span, :], preferred_element_type=F32)
        proj = term if proj is None else proj + term

    def rotated(values):
        return (values * cosine + pltpu.roll(values, half, 1) * sine).astype(BF16)

    heads = [rotated(proj[:, g * LANES : (g + 1) * LANES]) for g in range(group)]
    new_key = rotated(proj[:, group * LANES : (group + 1) * LANES])
    new_value = proj[:, (group + 1) * LANES :].astype(BF16)
    query = jnp.concatenate(heads, axis=0)

    scale = 1.0 / math.sqrt(LANES)
    load_pool.wait()
    scores = lax.dot_general(
        query, pool[:, :LANES], (((1,), (1,)), ((), ())), preferred_element_type=F32
    )
    offset = lax.rem(lane, page).astype(F32)
    masked = []
    for block in range(tokens // LANES):
        live = live_tokens[block * rows : (block + 1) * rows] > offset
        piece = scores[:, block * LANES : (block + 1) * LANES] * scale
        masked.append(
            jnp.concatenate(
                [
                    jnp.where(live, piece[g * rows : (g + 1) * rows], -jnp.inf)
                    for g in range(group)
                ],
                axis=0,
            )
        )
    scores = jnp.concatenate(masked, axis=1)
    keys = jnp.concatenate([new_key] * group, axis=0).astype(F32)
    values = jnp.concatenate([new_value] * group, axis=0).astype(F32)
    score_new = jnp.sum(query.astype(F32) * keys, axis=1, keepdims=True) * scale
    top = jnp.maximum(jnp.max(scores, axis=1, keepdims=True), score_new)
    weights = jnp.exp(scores - top)
    weight_new = jnp.exp(score_new - top)
    total = jnp.sum(weights, axis=1, keepdims=True) + weight_new
    numer = jnp.dot(weights.astype(BF16), pool[:, LANES:], preferred_element_type=F32)
    numer = numer + weight_new.astype(BF16).astype(F32) * values
    attn = (numer / total).astype(BF16)
    attn = jnp.concatenate([attn[g * rows : (g + 1) * rows] for g in range(group)], axis=1)

    load_wout.wait()
    pl.semaphore_wait(barrier, n - 1 + tp - 1)

    def columns(part):
        return pl.ds(pl.multiple_of(part * chunk, chunk), chunk)

    def part_copy(slot, landing, peer):
        return pltpu.make_async_remote_copy(
            src_ref=parts.at[slot],
            dst_ref=arrived.at[landing],
            send_sem=part_send.at[slot],
            recv_sem=part_recv.at[landing],
            device_id={"req": me, "tp": peer},
            device_id_type=MESH,
        )

    for shift in range(1, tp):
        peer = lax.rem(my_part + shift, tp)
        parts[peer] = jnp.dot(attn, wout[:, columns(peer)], preferred_element_type=F32)
        part_copy(peer, my_part, peer).start()
    summed = jnp.dot(attn, wout[:, columns(my_part)], preferred_element_type=F32)
    for shift in range(1, tp):
        peer = lax.rem(my_part + shift, tp)
        part_copy(peer, peer, peer).wait_recv()
        summed = summed + arrived[peer]
    mixed = (state_ref[:, columns(my_part)].astype(F32) + summed).astype(BF16)

    stacked = jnp.concatenate(
        [mixed[:, b * LANES : (b + 1) * LANES] for b in range(blocks)], axis=0
    )
    packed = jnp.dot(pack, stacked, preferred_element_type=F32)
    outgoing[...] = packed.reshape(n, 2 * blocks, LANES).astype(BF16)

    def send(shift, carry):
        peer = lax.rem(me + shift, n)
        pltpu.make_async_remote_copy(
            src_ref=outgoing.at[peer],
            dst_ref=incoming.at[me],
            send_sem=move_send,
            recv_sem=move_recv,
            device_id={"req": peer, "tp": my_part},
            device_id_type=MESH,
        ).start()
        return carry

    lax.fori_loop(1, n, send, 0)
    incoming[me] = outgoing[me]
    all_but_one = pl.ds(0, n - 1)
    pltpu.make_async_copy(
        outgoing.at[all_but_one], incoming.at[all_but_one], move_recv
    ).wait()
    received = incoming[...].astype(F32).reshape(total_rows, LANES).astype(BF16)
    moved = jnp.dot(unpack, received, preferred_element_type=F32).astype(BF16)
    share = jnp.concatenate(
        [moved[b * rows : (b + 1) * rows] for b in range(blocks)], axis=1
    )

    gathered[my_part] = share

    def gather_copy(landing, peer, slot):
        return pltpu.make_async_remote_copy(
            src_ref=gathered.at[landing],
            dst_ref=gathered.at[landing],
            send_sem=gather_send.at[slot],
            recv_sem=gather_recv.at[landing],
            device_id={"req": me, "tp": peer},
            device_id_type=MESH,
        )

    for shift in range(1, tp):
        peer = lax.rem(my_part + shift, tp)
        gather_copy(my_part, peer, shift).start()
    out_ref[:, columns(my_part)] = share
    for shift in range(1, tp):
        peer = lax.rem(my_part + shift, tp)
        gather_copy(peer, peer, shift).wait_recv()
        out_ref[:, columns(peer)] = gathered[peer]
    for shift in range(1, tp):
        peer = lax.rem(my_part + shift, tp)
        gather_copy(my_part, peer, shift).wait_send()
        part_copy(peer, my_part, peer).wait_send()
    pltpu.make_async_copy(
        outgoing.at[all_but_one], incoming.at[all_but_one], move_send
    ).wait()


def local(n, tp, state, norm_gain, w_qkv, w_out, kv_cache, lengths, page_table, dest_slot):
    rows, width = state.shape
    page_count, _, page, entry = kv_cache.shape
    tokens = page_count * page
    chunk = width // tp
    blocks = chunk // LANES
    vmem = pl.BlockSpec(memory_space=pltpu.VMEM)
    hbm = pl.BlockSpec(memory_space=pltpu.HBM)
    return pl.pallas_call(
        functools.partial(kernel, n, tp, page),
        out_shape=jax.ShapeDtypeStruct((rows, width), BF16),
        in_specs=[vmem, vmem, hbm, hbm, hbm, vmem, vmem, vmem],
        out_specs=vmem,
        scratch_shapes=[
            pltpu.VMEM((width, w_qkv.shape[2]), BF16),
            pltpu.VMEM((w_out.shape[1], width), BF16),
            pltpu.VMEM((tokens, entry), BF16),
            pltpu.VMEM((tp, rows, chunk), F32),
            pltpu.VMEM((tp, rows, chunk), F32),
            pltpu.VMEM((n, 2 * blocks, LANES), BF16),
            pltpu.VMEM((n, 2 * blocks, LANES), BF16),
            pltpu.VMEM((tp, rows, chunk), BF16),
            pltpu.SemaphoreType.DMA((6,)),
            pltpu.SemaphoreType.DMA((tp,)),
            pltpu.SemaphoreType.DMA((tp,)),
            pltpu.SemaphoreType.DMA,
            pltpu.SemaphoreType.DMA,
            pltpu.SemaphoreType.DMA((tp,)),
            pltpu.SemaphoreType.DMA((tp,)),
        ],
        compiler_params=pltpu.CompilerParams(
            collective_id=0, has_side_effects=True, vmem_limit_bytes=32 * 1024 * 1024
        ),
    )(
        state,
        norm_gain.reshape(1, width),
        w_qkv.reshape(width, w_qkv.shape[2]),
        w_out[0],
        kv_cache.reshape(tokens, entry),
        lengths.reshape(1, rows),
        page_table,
        dest_slot.reshape(1, rows),
    )


def solution(mesh):
    placed = (
        P("req", None),
        P(),
        P(None, "tp", None),
        P("tp", None, None),
        P("req", "tp", None, None),
        P("req"),
        P("req", None),
        P("req"),
    )
    return jax.shard_map(
        functools.partial(local, mesh.shape["req"], mesh.shape["tp"]),
        mesh=mesh,
        in_specs=placed,
        out_specs=P("req", None),
        check_vma=False,
    )
```

```python
import functools
import math

import jax
import jax.numpy as jnp
from jax import lax
from jax.experimental import pallas as pl
from jax.experimental.pallas import tpu as pltpu
from jax.sharding import PartitionSpec as P

MESH = pl.DeviceIdType.MESH
LANES = 128
F32 = jnp.float32
BF16 = jnp.bfloat16


def iota(shape, axis):
    return lax.broadcasted_iota(jnp.int32, shape, axis)


def to_column(row):
    size = row.shape[1]
    eye = iota((size, size), 0) == iota((size, size), 1)
    return jnp.sum(jnp.where(eye, jnp.broadcast_to(row, (size, size)), 0.0), axis=1, keepdims=True)


def kernel(
    n,
    tp,
    page,
    state_hbm,
    gain_hbm,
    wqkv_hbm,
    wout_hbm,
    pool_hbm,
    len_hbm,
    table_hbm,
    dest_hbm,
    out_ref,
    state_ref,
    gain_ref,
    len_ref,
    table_ref,
    dest_ref,
    wqkv,
    wout,
    pool,
    parts,
    arrived,
    outgoing,
    incoming,
    gathered,
    load_sem,
    part_send,
    part_recv,
    move_send,
    move_recv,
    gather_send,
    gather_recv,
):
    rows, width = state_ref.shape
    group = wout.shape[0] // LANES
    chunk = width // tp
    blocks = chunk // LANES
    tokens = pool.shape[0]
    page_count = tokens // page
    me = lax.axis_index("req")
    my_part = lax.axis_index("tp")

    steps = 4
    depth = width // steps
    loads = []
    for step in range(steps):
        span = pl.ds(step * depth, depth)
        loads.append(pltpu.make_async_copy(wqkv_hbm.at[span], wqkv.at[span], load_sem.at[step]))
    load_pool = pltpu.make_async_copy(pool_hbm, pool, load_sem.at[steps])
    load_wout = pltpu.make_async_copy(wout_hbm, wout, load_sem.at[steps + 1])
    small = []
    for slot, (src, dst) in enumerate(
        (
            (state_hbm, state_ref),
            (gain_hbm, gain_ref),
            (len_hbm, len_ref),
            (table_hbm, table_ref),
            (dest_hbm, dest_ref),
        )
    ):
        small.append(pltpu.make_async_copy(src, dst, load_sem.at[steps + 2 + slot]))
    for load in small + loads:
        load.start()
    load_pool.start()
    load_wout.start()

    barrier = pltpu.get_barrier_semaphore()

    def greet(shift, carry):
        pl.semaphore_signal(
            barrier,
            inc=1,
            device_id={"req": lax.rem(me + shift, n), "tp": my_part},
            device_id_type=MESH,
        )
        return carry

    lax.fori_loop(1, n, greet, 0)
    for shift in range(1, tp):
        pl.semaphore_signal(
            barrier,
            inc=1,
            device_id={"req": me, "tp": lax.rem(my_part + shift, tp)},
            device_id_type=MESH,
        )

    for load in small:
        load.wait()

    wide = state_ref[...].astype(F32)
    factor = lax.rsqrt(jnp.mean(wide * wide, axis=-1, keepdims=True) + 1e-05)
    normed = (wide * factor * gain_ref[...]).astype(BF16)

    length = to_column(len_ref[...].astype(F32))
    lane = iota((rows, LANES), 1)
    half = LANES // 2
    index = lax.rem(lane, half).astype(F32)
    freqs = jnp.exp(-math.log(1000000.0) * 2.0 * index / LANES)
    angles = length * freqs
    cosine = jnp.cos(angles)
    sine = jnp.sin(angles)
    sine = jnp.where(lane < half, -sine, sine)

    used = jnp.floor((length + (page - 1)) / page).astype(jnp.int32)
    table = table_ref[...]
    table = jnp.where(iota(table.shape, 1) < used, table, -1)
    padded = pl.cdiv(page_count, LANES) * LANES
    page_id = iota((rows, padded), 1)
    live_count = jnp.zeros((rows, padded), F32)
    for entry in range(table.shape[1]):
        left = length - float(entry * page)
        live_count = jnp.where(page_id == table[:, entry : entry + 1], left, live_count)
    live_count = jnp.clip(live_count, 0.0, float(page))
    per_block = LANES // page
    shifted = []
    for block in range(tokens // LANES):
        first = block * per_block
        base = first // LANES * LANES
        piece = live_count[:, base : base + LANES]
        if first != base:
            piece = pltpu.roll(piece, LANES - (first - base), 1)
        shifted.append(piece)
    spread = (iota((LANES, LANES), 0) == iota((LANES, LANES), 1) // page).astype(BF16)
    live_tokens = jnp.dot(
        jnp.concatenate(shifted, axis=0).astype(BF16), spread, preferred_element_type=F32
    )

    shift_bits = rows.bit_length() - 1
    target_row = lax.shift_right_logical(dest_ref[...], shift_bits).astype(F32)
    target = to_column(target_row)
    same = jnp.broadcast_to(target, (rows, rows)) == jnp.broadcast_to(target_row, (rows, rows))
    earlier = iota((rows, rows), 1) < iota((rows, rows), 0)
    rank = jnp.sum(jnp.where(same & earlier, 1.0, 0.0), axis=1, keepdims=True)
    source = (2 * me).astype(F32) - target
    source = jnp.where(source < 0, source + n, source)
    source = jnp.where(source >= n, source - n, source)
    key_out = (target * 2 + rank).astype(jnp.int32)
    key_in = (source * 2 + rank).astype(jnp.int32)
    flat = rows * blocks
    total_rows = n * 2 * blocks
    picked = iota((rows, flat), 0) == lax.rem(iota((rows, flat), 1), rows)
    key_row = jnp.sum(jnp.where(picked, key_out, 0).astype(F32), axis=0, keepdims=True).astype(
        jnp.int32
    )
    row_id = iota((total_rows, flat), 0)
    col_id = iota((total_rows, flat), 1)
    pack = (
        (row_id // blocks == key_row) & (lax.rem(row_id, blocks) == col_id // rows)
    ).astype(BF16)
    key_col = jnp.concatenate([key_in] * blocks, axis=0)
    row_id = iota((flat, total_rows), 0)
    col_id = iota((flat, total_rows), 1)
    unpack = (
        (col_id // blocks == key_col) & (lax.rem(col_id, blocks) == row_id // rows)
    ).astype(BF16)

    proj = None
    for step in range(steps):
        loads[step].wait()
        span = slice(step * depth, (step + 1) * depth)
        term = jnp.dot(normed[:, span], wqkv[span, :], preferred_element_type=F32)
        proj = term if proj is None else proj + term

    def rotated(values):
        return (values * cosine + pltpu.roll(values, half, 1) * sine).astype(BF16)

    heads = [rotated(proj[:, g * LANES : (g + 1) * LANES]) for g in range(group)]
    new_key = rotated(proj[:, group * LANES : (group + 1) * LANES])
    new_value = proj[:, (group + 1) * LANES :].astype(BF16)
    query = jnp.concatenate(heads, axis=0)

    scale = 1.0 / math.sqrt(LANES)
    load_pool.wait()
    scores = lax.dot_general(
        query, pool[:, :LANES], (((1,), (1,)), ((), ())), preferred_element_type=F32
    )
    offset = lax.rem(lane, page).astype(F32)
    masked = []
    for block in range(tokens // LANES):
        live = live_tokens[block * rows : (block + 1) * rows] > offset
        piece = scores[:, block * LANES : (block + 1) * LANES] * scale
        masked.append(
            jnp.concatenate(
                [
                    jnp.where(live, piece[g * rows : (g + 1) * rows], -jnp.inf)
                    for g in range(group)
                ],
                axis=0,
            )
        )
    scores = jnp.concatenate(masked, axis=1)
    keys = jnp.concatenate([new_key] * group, axis=0).astype(F32)
    values = jnp.concatenate([new_value] * group, axis=0).astype(F32)
    score_new = jnp.sum(query.astype(F32) * keys, axis=1, keepdims=True) * scale
    top = jnp.maximum(jnp.max(scores, axis=1, keepdims=True), score_new)
    weights = jnp.exp(scores - top)
    weight_new = jnp.exp(score_new - top)
    total = jnp.sum(weights, axis=1, keepdims=True) + weight_new
    numer = jnp.dot(weights.astype(BF16), pool[:, LANES:], preferred_element_type=F32)
    numer = numer + weight_new.astype(BF16).astype(F32) * values
    attn = (numer / total).astype(BF16)
    attn = jnp.concatenate([attn[g * rows : (g + 1) * rows] for g in range(group)], axis=1)

    load_wout.wait()
    pl.semaphore_wait(barrier, n - 1 + tp - 1)

    def columns(part):
        return pl.ds(pl.multiple_of(part * chunk, chunk), chunk)

    def part_copy(slot, landing, peer):
        return pltpu.make_async_remote_copy(
            src_ref=parts.at[slot],
            dst_ref=arrived.at[landing],
            send_sem=part_send.at[slot],
            recv_sem=part_recv.at[landing],
            device_id={"req": me, "tp": peer},
            device_id_type=MESH,
        )

    for shift in range(1, tp):
        peer = lax.rem(my_part + shift, tp)
        parts[peer] = jnp.dot(attn, wout[:, columns(peer)], preferred_element_type=F32)
        part_copy(peer, my_part, peer).start()
    summed = jnp.dot(attn, wout[:, columns(my_part)], preferred_element_type=F32)
    for shift in range(1, tp):
        peer = lax.rem(my_part + shift, tp)
        part_copy(peer, peer, peer).wait_recv()
        summed = summed + arrived[peer]
    mixed = (state_ref[:, columns(my_part)].astype(F32) + summed).astype(BF16)

    stacked = jnp.concatenate(
        [mixed[:, b * LANES : (b + 1) * LANES] for b in range(blocks)], axis=0
    )
    packed = jnp.dot(pack, stacked, preferred_element_type=F32)
    outgoing[...] = packed.reshape(n, 2 * blocks, LANES).astype(BF16)

    def send(shift, carry):
        peer = lax.rem(me + shift, n)
        pltpu.make_async_remote_copy(
            src_ref=outgoing.at[peer],
            dst_ref=incoming.at[me],
            send_sem=move_send,
            recv_sem=move_recv,
            device_id={"req": peer, "tp": my_part},
            device_id_type=MESH,
        ).start()
        return carry

    lax.fori_loop(1, n, send, 0)
    incoming[me] = outgoing[me]
    all_but_one = pl.ds(0, n - 1)
    pltpu.make_async_copy(
        outgoing.at[all_but_one], incoming.at[all_but_one], move_recv
    ).wait()
    received = incoming[...].astype(F32).reshape(total_rows, LANES).astype(BF16)
    moved = jnp.dot(unpack, received, preferred_element_type=F32).astype(BF16)
    share = jnp.concatenate(
        [moved[b * rows : (b + 1) * rows] for b in range(blocks)], axis=1
    )

    gathered[my_part] = share

    def gather_copy(landing, peer, slot):
        return pltpu.make_async_remote_copy(
            src_ref=gathered.at[landing],
            dst_ref=gathered.at[landing],
            send_sem=gather_send.at[slot],
            recv_sem=gather_recv.at[landing],
            device_id={"req": me, "tp": peer},
            device_id_type=MESH,
        )

    for shift in range(1, tp):
        peer = lax.rem(my_part + shift, tp)
        gather_copy(my_part, peer, shift).start()
    out_ref[:, columns(my_part)] = share
    for shift in range(1, tp):
        peer = lax.rem(my_part + shift, tp)
        gather_copy(peer, peer, shift).wait_recv()
        out_ref[:, columns(peer)] = gathered[peer]
    for shift in range(1, tp):
        peer = lax.rem(my_part + shift, tp)
        gather_copy(my_part, peer, shift).wait_send()
        part_copy(peer, my_part, peer).wait_send()
    pltpu.make_async_copy(
        outgoing.at[all_but_one], incoming.at[all_but_one], move_send
    ).wait()


def local(n, tp, state, norm_gain, w_qkv, w_out, kv_cache, lengths, page_table, dest_slot):
    rows, width = state.shape
    page_count, _, page, entry = kv_cache.shape
    tokens = page_count * page
    chunk = width // tp
    blocks = chunk // LANES
    vmem = pl.BlockSpec(memory_space=pltpu.VMEM)
    hbm = pl.BlockSpec(memory_space=pltpu.HBM)
    return pl.pallas_call(
        functools.partial(kernel, n, tp, page),
        out_shape=jax.ShapeDtypeStruct((rows, width), BF16),
        in_specs=[hbm] * 8,
        out_specs=vmem,
        scratch_shapes=[
            pltpu.VMEM((rows, width), BF16),
            pltpu.VMEM((1, width), F32),
            pltpu.VMEM((1, rows), jnp.int32),
            pltpu.VMEM(page_table.shape, jnp.int32),
            pltpu.VMEM((1, rows), jnp.int32),
            pltpu.VMEM((width, w_qkv.shape[2]), BF16),
            pltpu.VMEM((w_out.shape[1], width), BF16),
            pltpu.VMEM((tokens, entry), BF16),
            pltpu.VMEM((tp, rows, chunk), F32),
            pltpu.VMEM((tp, rows, chunk), F32),
            pltpu.VMEM((n, 2 * blocks, LANES), BF16),
            pltpu.VMEM((n, 2 * blocks, LANES), BF16),
            pltpu.VMEM((tp, rows, chunk), BF16),
            pltpu.SemaphoreType.DMA((11,)),
            pltpu.SemaphoreType.DMA((tp,)),
            pltpu.SemaphoreType.DMA((tp,)),
            pltpu.SemaphoreType.DMA,
            pltpu.SemaphoreType.DMA,
            pltpu.SemaphoreType.DMA((tp,)),
            pltpu.SemaphoreType.DMA((tp,)),
        ],
        compiler_params=pltpu.CompilerParams(
            collective_id=0, has_side_effects=True, vmem_limit_bytes=60 * 1024 * 1024
        ),
    )(
        state,
        norm_gain.reshape(1, width),
        w_qkv.reshape(width, w_qkv.shape[2]),
        w_out[0],
        kv_cache.reshape(tokens, entry),
        lengths.reshape(1, rows),
        page_table,
        dest_slot.reshape(1, rows),
    )


def solution(mesh):
    placed = (
        P("req", None),
        P(),
        P(None, "tp", None),
        P("tp", None, None),
        P("req", "tp", None, None),
        P("req"),
        P("req", None),
        P("req"),
    )
    return jax.shard_map(
        functools.partial(local, mesh.shape["req"], mesh.shape["tp"]),
        mesh=mesh,
        in_specs=placed,
        out_specs=P("req", None),
        check_vma=False,
    )
```

```python
import functools
import math

import jax
import jax.numpy as jnp
from jax import lax
from jax.experimental import pallas as pl
from jax.experimental.pallas import tpu as pltpu
from jax.sharding import PartitionSpec as P

MESH = pl.DeviceIdType.MESH
LANES = 128
F32 = jnp.float32
BF16 = jnp.bfloat16


def iota(shape, axis):
    return lax.broadcasted_iota(jnp.int32, shape, axis)


def to_column(row):
    size = row.shape[1]
    eye = iota((size, size), 0) == iota((size, size), 1)
    return jnp.sum(jnp.where(eye, jnp.broadcast_to(row, (size, size)), 0.0), axis=1, keepdims=True)


def kernel(
    n,
    tp,
    page,
    state_hbm,
    gain_hbm,
    wqkv_hbm,
    wout_hbm,
    pool_hbm,
    len_hbm,
    table_hbm,
    dest_hbm,
    out_ref,
    state_ref,
    gain_ref,
    len_ref,
    table_ref,
    dest_ref,
    wqkv,
    wout,
    pool,
    parts,
    arrived,
    outgoing,
    incoming,
    load_sem,
    part_send,
    part_recv,
    move_send,
    move_recv,
):
    rows, width = state_ref.shape
    group = wout.shape[0] // LANES
    chunk = width // tp
    blocks = chunk // LANES
    tokens = pool.shape[0]
    page_count = tokens // page
    me = lax.axis_index("req")
    my_part = lax.axis_index("tp")

    steps = 4
    depth = width // steps
    loads = []
    for step in range(steps):
        span = pl.ds(step * depth, depth)
        loads.append(pltpu.make_async_copy(wqkv_hbm.at[span], wqkv.at[span], load_sem.at[step]))
    load_pool = pltpu.make_async_copy(pool_hbm, pool, load_sem.at[steps])
    load_wout = pltpu.make_async_copy(wout_hbm, wout, load_sem.at[steps + 1])
    small = []
    for slot, (src, dst) in enumerate(
        (
            (state_hbm, state_ref),
            (gain_hbm, gain_ref),
            (len_hbm, len_ref),
            (table_hbm, table_ref),
            (dest_hbm, dest_ref),
        )
    ):
        small.append(pltpu.make_async_copy(src, dst, load_sem.at[steps + 2 + slot]))
    for load in small + loads:
        load.start()
    load_pool.start()
    load_wout.start()

    barrier = pltpu.get_barrier_semaphore()

    def partner(step):
        other = lax.rem(my_part * n + me + step, n * tp)
        return {"req": lax.rem(other, n), "tp": other // n}

    def greet(step, carry):
        pl.semaphore_signal(barrier, inc=1, device_id=partner(step), device_id_type=MESH)
        return carry

    lax.fori_loop(1, n * tp, greet, 0)

    for load in small:
        load.wait()

    wide = state_ref[...].astype(F32)
    factor = lax.rsqrt(jnp.mean(wide * wide, axis=-1, keepdims=True) + 1e-05)
    normed = (wide * factor * gain_ref[...]).astype(BF16)

    length = to_column(len_ref[...].astype(F32))
    lane = iota((rows, LANES), 1)
    half = LANES // 2
    index = lax.rem(lane, half).astype(F32)
    freqs = jnp.exp(-math.log(1000000.0) * 2.0 * index / LANES)
    angles = length * freqs
    cosine = jnp.cos(angles)
    sine = jnp.sin(angles)
    sine = jnp.where(lane < half, -sine, sine)

    used = jnp.floor((length + (page - 1)) / page).astype(jnp.int32)
    table = table_ref[...]
    table = jnp.where(iota(table.shape, 1) < used, table, -1)
    padded = pl.cdiv(page_count, LANES) * LANES
    page_id = iota((rows, padded), 1)
    live_count = jnp.zeros((rows, padded), F32)
    for entry in range(table.shape[1]):
        left = length - float(entry * page)
        live_count = jnp.where(page_id == table[:, entry : entry + 1], left, live_count)
    live_count = jnp.clip(live_count, 0.0, float(page))
    per_block = LANES // page
    shifted = []
    for block in range(tokens // LANES):
        first = block * per_block
        base = first // LANES * LANES
        piece = live_count[:, base : base + LANES]
        if first != base:
            piece = pltpu.roll(piece, LANES - (first - base), 1)
        shifted.append(piece)
    spread = (iota((LANES, LANES), 0) == iota((LANES, LANES), 1) // page).astype(BF16)
    live_tokens = jnp.dot(
        jnp.concatenate(shifted, axis=0).astype(BF16), spread, preferred_element_type=F32
    )

    shift_bits = rows.bit_length() - 1
    target_row = lax.shift_right_logical(dest_ref[...], shift_bits).astype(F32)
    target = to_column(target_row)
    same = jnp.broadcast_to(target, (rows, rows)) == jnp.broadcast_to(target_row, (rows, rows))
    earlier = iota((rows, rows), 1) < iota((rows, rows), 0)
    rank = jnp.sum(jnp.where(same & earlier, 1.0, 0.0), axis=1, keepdims=True)
    source = (2 * me).astype(F32) - target
    source = jnp.where(source < 0, source + n, source)
    source = jnp.where(source >= n, source - n, source)
    key_out = (target * 2 + rank).astype(jnp.int32)
    key_in = (source * 2 + rank).astype(jnp.int32)
    flat = rows * blocks
    total_rows = n * 2 * blocks
    picked = iota((rows, flat), 0) == lax.rem(iota((rows, flat), 1), rows)
    key_row = jnp.sum(jnp.where(picked, key_out, 0).astype(F32), axis=0, keepdims=True).astype(
        jnp.int32
    )
    row_id = iota((total_rows, flat), 0)
    col_id = iota((total_rows, flat), 1)
    pack = (
        (row_id // blocks == key_row) & (lax.rem(row_id, blocks) == col_id // rows)
    ).astype(BF16)
    key_col = jnp.concatenate([key_in] * blocks, axis=0)
    row_id = iota((flat, total_rows), 0)
    col_id = iota((flat, total_rows), 1)
    unpack = (
        (col_id // blocks == key_col) & (lax.rem(col_id, blocks) == row_id // rows)
    ).astype(BF16)

    proj = None
    for step in range(steps):
        loads[step].wait()
        span = slice(step * depth, (step + 1) * depth)
        term = jnp.dot(normed[:, span], wqkv[span, :], preferred_element_type=F32)
        proj = term if proj is None else proj + term

    def rotated(values):
        return (values * cosine + pltpu.roll(values, half, 1) * sine).astype(BF16)

    heads = [rotated(proj[:, g * LANES : (g + 1) * LANES]) for g in range(group)]
    new_key = rotated(proj[:, group * LANES : (group + 1) * LANES])
    new_value = proj[:, (group + 1) * LANES :].astype(BF16)
    query = jnp.concatenate(heads, axis=0)

    scale = 1.0 / math.sqrt(LANES)
    load_pool.wait()
    scores = lax.dot_general(
        query, pool[:, :LANES], (((1,), (1,)), ((), ())), preferred_element_type=F32
    )
    offset = lax.rem(lane, page).astype(F32)
    masked = []
    for block in range(tokens // LANES):
        live = live_tokens[block * rows : (block + 1) * rows] > offset
        piece = scores[:, block * LANES : (block + 1) * LANES] * scale
        masked.append(
            jnp.concatenate(
                [
                    jnp.where(live, piece[g * rows : (g + 1) * rows], -jnp.inf)
                    for g in range(group)
                ],
                axis=0,
            )
        )
    scores = jnp.concatenate(masked, axis=1)
    keys = jnp.concatenate([new_key] * group, axis=0).astype(F32)
    values = jnp.concatenate([new_value] * group, axis=0).astype(F32)
    score_new = jnp.sum(query.astype(F32) * keys, axis=1, keepdims=True) * scale
    top = jnp.maximum(jnp.max(scores, axis=1, keepdims=True), score_new)
    weights = jnp.exp(scores - top)
    weight_new = jnp.exp(score_new - top)
    total = jnp.sum(weights, axis=1, keepdims=True) + weight_new
    numer = jnp.dot(weights.astype(BF16), pool[:, LANES:], preferred_element_type=F32)
    numer = numer + weight_new.astype(BF16).astype(F32) * values
    attn = (numer / total).astype(BF16)
    attn = jnp.concatenate([attn[g * rows : (g + 1) * rows] for g in range(group)], axis=1)

    load_wout.wait()
    pl.semaphore_wait(barrier, n * tp - 1)

    def columns(part):
        return pl.ds(pl.multiple_of(part * chunk, chunk), chunk)

    def part_copy(slot, landing, peer):
        return pltpu.make_async_remote_copy(
            src_ref=parts.at[slot],
            dst_ref=arrived.at[landing],
            send_sem=part_send.at[slot],
            recv_sem=part_recv.at[landing],
            device_id={"req": me, "tp": peer},
            device_id_type=MESH,
        )

    for shift in range(1, tp):
        peer = lax.rem(my_part + shift, tp)
        parts[peer] = jnp.dot(
            attn, wout[:, columns(peer)], preferred_element_type=F32
        ).astype(BF16)
        part_copy(peer, my_part, peer).start()
    summed = jnp.dot(attn, wout[:, columns(my_part)], preferred_element_type=F32)
    for shift in range(1, tp):
        peer = lax.rem(my_part + shift, tp)
        part_copy(peer, peer, peer).wait_recv()
        summed = summed + arrived[peer].astype(F32)
    mixed = (state_ref[:, columns(my_part)].astype(F32) + summed).astype(BF16)

    stacked = jnp.concatenate(
        [mixed[:, b * LANES : (b + 1) * LANES] for b in range(blocks)], axis=0
    )
    packed = jnp.dot(pack, stacked, preferred_element_type=F32)
    outgoing[...] = packed.reshape(n, 2 * blocks, LANES).astype(BF16)

    def send(step, carry):
        place = partner(step)
        pltpu.make_async_remote_copy(
            src_ref=outgoing.at[place["req"]],
            dst_ref=incoming.at[my_part * n + me],
            send_sem=move_send,
            recv_sem=move_recv,
            device_id=place,
            device_id_type=MESH,
        ).start()
        return carry

    lax.fori_loop(1, n * tp, send, 0)
    incoming[my_part * n + me] = outgoing[me]
    all_but_one = incoming.at[pl.ds(0, n * tp - 1)]
    pltpu.make_async_copy(all_but_one, all_but_one, move_recv).wait()
    for part in range(tp):
        received = incoming[part * n : (part + 1) * n].astype(F32)
        received = received.reshape(total_rows, LANES).astype(BF16)
        moved = jnp.dot(unpack, received, preferred_element_type=F32).astype(BF16)
        for b in range(blocks):
            first = part * chunk + b * LANES
            out_ref[:, first : first + LANES] = moved[b * rows : (b + 1) * rows]
    for shift in range(1, tp):
        peer = lax.rem(my_part + shift, tp)
        part_copy(peer, my_part, peer).wait_send()
    pltpu.make_async_copy(all_but_one, all_but_one, move_send).wait()


def local(n, tp, state, norm_gain, w_qkv, w_out, kv_cache, lengths, page_table, dest_slot):
    rows, width = state.shape
    page_count, _, page, entry = kv_cache.shape
    tokens = page_count * page
    chunk = width // tp
    blocks = chunk // LANES
    vmem = pl.BlockSpec(memory_space=pltpu.VMEM)
    hbm = pl.BlockSpec(memory_space=pltpu.HBM)
    return pl.pallas_call(
        functools.partial(kernel, n, tp, page),
        out_shape=pltpu.VMEM((rows, width), BF16),
        in_specs=[hbm] * 8,
        out_specs=vmem,
        scratch_shapes=[
            pltpu.VMEM((rows, width), BF16),
            pltpu.VMEM((1, width), F32),
            pltpu.VMEM((1, rows), jnp.int32),
            pltpu.VMEM(page_table.shape, jnp.int32),
            pltpu.VMEM((1, rows), jnp.int32),
            pltpu.VMEM((width, w_qkv.shape[2]), BF16),
            pltpu.VMEM((w_out.shape[1], width), BF16),
            pltpu.VMEM((tokens, entry), BF16),
            pltpu.VMEM((tp, rows, chunk), BF16),
            pltpu.VMEM((tp, rows, chunk), BF16),
            pltpu.VMEM((n, 2 * blocks, LANES), BF16),
            pltpu.VMEM((n * tp, 2 * blocks, LANES), BF16),
            pltpu.SemaphoreType.DMA((11,)),
            pltpu.SemaphoreType.DMA((tp,)),
            pltpu.SemaphoreType.DMA((tp,)),
            pltpu.SemaphoreType.DMA,
            pltpu.SemaphoreType.DMA,
        ],
        compiler_params=pltpu.CompilerParams(
            collective_id=0, has_side_effects=True, vmem_limit_bytes=60 * 1024 * 1024
        ),
    )(
        state,
        norm_gain.reshape(1, width),
        w_qkv.reshape(width, w_qkv.shape[2]),
        w_out[0],
        kv_cache.reshape(tokens, entry),
        lengths.reshape(1, rows),
        page_table,
        dest_slot.reshape(1, rows),
    )


def solution(mesh):
    placed = (
        P("req", None),
        P(),
        P(None, "tp", None),
        P("tp", None, None),
        P("req", "tp", None, None),
        P("req"),
        P("req", None),
        P("req"),
    )
    return jax.shard_map(
        functools.partial(local, mesh.shape["req"], mesh.shape["tp"]),
        mesh=mesh,
        in_specs=placed,
        out_specs=P("req", None),
        check_vma=False,
    )
```

```python
import functools
import math

import jax
import jax.numpy as jnp
from jax import lax
from jax.experimental import pallas as pl
from jax.experimental.pallas import tpu as pltpu
from jax.sharding import PartitionSpec as P

MESH = pl.DeviceIdType.MESH
LANES = 128
F32 = jnp.float32
BF16 = jnp.bfloat16


def iota(shape, axis):
    return lax.broadcasted_iota(jnp.int32, shape, axis)


def to_column(row):
    size = row.shape[1]
    eye = iota((size, size), 0) == iota((size, size), 1)
    return jnp.sum(jnp.where(eye, jnp.broadcast_to(row, (size, size)), 0.0), axis=1, keepdims=True)


def kernel(
    n,
    tp,
    page,
    state_hbm,
    gain_hbm,
    wqkv_hbm,
    wout_hbm,
    pool_hbm,
    len_hbm,
    table_hbm,
    dest_hbm,
    out_ref,
    state_ref,
    gain_ref,
    len_ref,
    table_ref,
    dest_ref,
    wqkv,
    wout,
    pool,
    outgoing,
    incoming,
    load_sem,
    move_send,
    move_recv,
):
    rows, width = state_ref.shape
    group = wout.shape[0] // LANES
    chunk = width // tp
    blocks = chunk // LANES
    tokens = pool.shape[0]
    page_count = tokens // page
    me = lax.axis_index("req")
    my_part = lax.axis_index("tp")

    steps = 4
    depth = width // steps
    loads = []
    for step in range(steps):
        span = pl.ds(step * depth, depth)
        loads.append(pltpu.make_async_copy(wqkv_hbm.at[span], wqkv.at[span], load_sem.at[step]))
    load_pool = pltpu.make_async_copy(pool_hbm, pool, load_sem.at[steps])
    load_wout = pltpu.make_async_copy(wout_hbm, wout, load_sem.at[steps + 1])
    small = []
    for slot, (src, dst) in enumerate(
        (
            (state_hbm, state_ref),
            (gain_hbm, gain_ref),
            (len_hbm, len_ref),
            (table_hbm, table_ref),
            (dest_hbm, dest_ref),
        )
    ):
        small.append(pltpu.make_async_copy(src, dst, load_sem.at[steps + 2 + slot]))
    for load in small + loads:
        load.start()
    load_pool.start()
    load_wout.start()

    barrier = pltpu.get_barrier_semaphore()

    def wrapped(value, size):
        return jnp.where(value >= size, value - size, value)

    def each_partner(act):
        def visit(shift, carry):
            peer = wrapped(me + shift, n)
            for part_shift in range(tp):
                if part_shift or not isinstance(shift, int) or shift:
                    act(peer, wrapped(my_part + part_shift, tp))
            return carry

        if n * tp <= 64:
            for shift in range(n):
                visit(shift, 0)
        else:
            for part_shift in range(1, tp):
                act(me, wrapped(my_part + part_shift, tp))
            lax.fori_loop(1, n, visit, 0)

    def greet(peer, part):
        pl.semaphore_signal(
            barrier, inc=1, device_id={"req": peer, "tp": part}, device_id_type=MESH
        )

    each_partner(greet)

    for load in small:
        load.wait()

    wide = state_ref[...].astype(F32)
    factor = lax.rsqrt(jnp.mean(wide * wide, axis=-1, keepdims=True) + 1e-05)
    normed = (wide * factor * gain_ref[...]).astype(BF16)

    length = to_column(len_ref[...].astype(F32))
    lane = iota((rows, LANES), 1)
    half = LANES // 2
    index = lax.rem(lane, half).astype(F32)
    freqs = jnp.exp(-math.log(1000000.0) * 2.0 * index / LANES)
    angles = length * freqs
    cosine = jnp.cos(angles)
    sine = jnp.sin(angles)
    sine = jnp.where(lane < half, -sine, sine)

    used = jnp.floor((length + (page - 1)) / page).astype(jnp.int32)
    table = table_ref[...]
    table = jnp.where(iota(table.shape, 1) < used, table, -1)
    padded = pl.cdiv(page_count, LANES) * LANES
    page_id = iota((rows, padded), 1)
    live_count = jnp.zeros((rows, padded), F32)
    for entry in range(table.shape[1]):
        left = length - float(entry * page)
        live_count = jnp.where(page_id == table[:, entry : entry + 1], left, live_count)
    live_count = jnp.clip(live_count, 0.0, float(page))
    per_block = LANES // page
    shifted = []
    for block in range(tokens // LANES):
        first = block * per_block
        base = first // LANES * LANES
        piece = live_count[:, base : base + LANES]
        if first != base:
            piece = pltpu.roll(piece, LANES - (first - base), 1)
        shifted.append(piece)
    spread = (iota((LANES, LANES), 0) == iota((LANES, LANES), 1) // page).astype(BF16)
    live_tokens = jnp.dot(
        jnp.concatenate(shifted, axis=0).astype(BF16), spread, preferred_element_type=F32
    )

    shift_bits = rows.bit_length() - 1
    target_row = lax.shift_right_logical(dest_ref[...], shift_bits).astype(F32)
    target = to_column(target_row)
    same = jnp.broadcast_to(target, (rows, rows)) == jnp.broadcast_to(target_row, (rows, rows))
    earlier = iota((rows, rows), 1) < iota((rows, rows), 0)
    rank = jnp.sum(jnp.where(same & earlier, 1.0, 0.0), axis=1, keepdims=True)
    source = (2 * me).astype(F32) - target
    source = jnp.where(source < 0, source + n, source)
    source = jnp.where(source >= n, source - n, source)
    key_out = (target * 2 + rank).astype(jnp.int32)
    key_in = (source * 2 + rank).astype(jnp.int32)
    flat = rows * blocks
    total_rows = n * 2 * blocks
    picked = iota((rows, flat), 0) == lax.rem(iota((rows, flat), 1), rows)
    key_row = jnp.sum(jnp.where(picked, key_out, 0).astype(F32), axis=0, keepdims=True).astype(
        jnp.int32
    )
    row_id = iota((total_rows, flat), 0)
    col_id = iota((total_rows, flat), 1)
    pack = (
        (row_id // blocks == key_row) & (lax.rem(row_id, blocks) == col_id // rows)
    ).astype(BF16)
    key_col = jnp.concatenate([key_in] * blocks, axis=0)
    row_id = iota((flat, total_rows), 0)
    col_id = iota((flat, total_rows), 1)
    unpack = (
        (col_id // blocks == key_col) & (lax.rem(col_id, blocks) == row_id // rows)
    ).astype(BF16)

    proj = None
    for step in range(steps):
        loads[step].wait()
        span = slice(step * depth, (step + 1) * depth)
        term = jnp.dot(normed[:, span], wqkv[span, :], preferred_element_type=F32)
        proj = term if proj is None else proj + term

    def rotated(values):
        return (values * cosine + pltpu.roll(values, half, 1) * sine).astype(BF16)

    heads = [rotated(proj[:, g * LANES : (g + 1) * LANES]) for g in range(group)]
    new_key = rotated(proj[:, group * LANES : (group + 1) * LANES])
    new_value = proj[:, (group + 1) * LANES :].astype(BF16)
    query = jnp.concatenate(heads, axis=0)

    scale = 1.0 / math.sqrt(LANES)
    load_pool.wait()
    scores = lax.dot_general(
        query, pool[:, :LANES], (((1,), (1,)), ((), ())), preferred_element_type=F32
    )
    offset = lax.rem(lane, page).astype(F32)
    masked = []
    for block in range(tokens // LANES):
        live = live_tokens[block * rows : (block + 1) * rows] > offset
        piece = scores[:, block * LANES : (block + 1) * LANES] * scale
        masked.append(
            jnp.concatenate(
                [
                    jnp.where(live, piece[g * rows : (g + 1) * rows], -jnp.inf)
                    for g in range(group)
                ],
                axis=0,
            )
        )
    scores = jnp.concatenate(masked, axis=1)
    keys = jnp.concatenate([new_key] * group, axis=0).astype(F32)
    values = jnp.concatenate([new_value] * group, axis=0).astype(F32)
    score_new = jnp.sum(query.astype(F32) * keys, axis=1, keepdims=True) * scale
    top = jnp.maximum(jnp.max(scores, axis=1, keepdims=True), score_new)
    weights = jnp.exp(scores - top)
    weight_new = jnp.exp(score_new - top)
    total = jnp.sum(weights, axis=1, keepdims=True) + weight_new
    numer = jnp.dot(weights.astype(BF16), pool[:, LANES:], preferred_element_type=F32)
    numer = numer + weight_new.astype(BF16).astype(F32) * values
    attn = (numer / total).astype(BF16)
    attn = jnp.concatenate([attn[g * rows : (g + 1) * rows] for g in range(group)], axis=1)

    load_wout.wait()
    own_state = (my_part == 0).astype(F32)
    term = jnp.dot(attn, wout[...], preferred_element_type=F32)
    mixed = (state_ref[...].astype(F32) * own_state + term).astype(BF16)

    piece_rows = 2 * blocks
    for part in range(tp):
        first = part * chunk
        stacked = jnp.concatenate(
            [mixed[:, first + b * LANES : first + (b + 1) * LANES] for b in range(blocks)], axis=0
        )
        packed = jnp.dot(pack, stacked, preferred_element_type=F32)
        outgoing[:, part * piece_rows : (part + 1) * piece_rows] = packed.reshape(
            n, piece_rows, LANES
        ).astype(BF16)
    pl.semaphore_wait(barrier, n * tp - 1)
    slot = my_part * n + me

    def send(peer, part):
        pltpu.make_async_remote_copy(
            src_ref=outgoing.at[peer],
            dst_ref=incoming.at[slot],
            send_sem=move_send,
            recv_sem=move_recv,
            device_id={"req": peer, "tp": part},
            device_id_type=MESH,
        ).start()

    each_partner(send)
    incoming[slot] = outgoing[me]
    all_but_one = incoming.at[pl.ds(0, n * tp - 1)]
    pltpu.make_async_copy(all_but_one, all_but_one, move_recv).wait()
    for part in range(tp):
        moved = None
        for origin in range(tp):
            received = incoming[
                origin * n : (origin + 1) * n, part * piece_rows : (part + 1) * piece_rows
            ].astype(F32)
            received = received.reshape(total_rows, LANES).astype(BF16)
            taken = jnp.dot(unpack, received, preferred_element_type=F32)
            moved = taken if moved is None else moved + taken
        moved = moved.astype(BF16)
        for b in range(blocks):
            first = part * chunk + b * LANES
            out_ref[:, first : first + LANES] = moved[b * rows : (b + 1) * rows]
    pltpu.make_async_copy(all_but_one, all_but_one, move_send).wait()


def local(n, tp, state, norm_gain, w_qkv, w_out, kv_cache, lengths, page_table, dest_slot):
    rows, width = state.shape
    page_count, _, page, entry = kv_cache.shape
    tokens = page_count * page
    chunk = width // tp
    blocks = chunk // LANES
    vmem = pl.BlockSpec(memory_space=pltpu.VMEM)
    hbm = pl.BlockSpec(memory_space=pltpu.HBM)
    return pl.pallas_call(
        functools.partial(kernel, n, tp, page),
        out_shape=pltpu.VMEM((rows, width), BF16),
        in_specs=[hbm] * 8,
        out_specs=vmem,
        scratch_shapes=[
            pltpu.VMEM((rows, width), BF16),
            pltpu.VMEM((1, width), F32),
            pltpu.VMEM((1, rows), jnp.int32),
            pltpu.VMEM(page_table.shape, jnp.int32),
            pltpu.VMEM((1, rows), jnp.int32),
            pltpu.VMEM((width, w_qkv.shape[2]), BF16),
            pltpu.VMEM((w_out.shape[1], width), BF16),
            pltpu.VMEM((tokens, entry), BF16),
            pltpu.VMEM((n, 2 * blocks * tp, LANES), BF16),
            pltpu.VMEM((n * tp, 2 * blocks * tp, LANES), BF16),
            pltpu.SemaphoreType.DMA((11,)),
            pltpu.SemaphoreType.DMA,
            pltpu.SemaphoreType.DMA,
        ],
        compiler_params=pltpu.CompilerParams(
            collective_id=0, has_side_effects=True, vmem_limit_bytes=60 * 1024 * 1024
        ),
    )(
        state,
        norm_gain.reshape(1, width),
        w_qkv.reshape(width, w_qkv.shape[2]),
        w_out[0],
        kv_cache.reshape(tokens, entry),
        lengths.reshape(1, rows),
        page_table,
        dest_slot.reshape(1, rows),
    )


def solution(mesh):
    placed = (
        P("req", None),
        P(),
        P(None, "tp", None),
        P("tp", None, None),
        P("req", "tp", None, None),
        P("req"),
        P("req", None),
        P("req"),
    )
    return jax.shard_map(
        functools.partial(local, mesh.shape["req"], mesh.shape["tp"]),
        mesh=mesh,
        in_specs=placed,
        out_specs=P("req", None),
        check_vma=False,
    )
```

```python
import functools
import math

import jax
import jax.numpy as jnp
from jax import lax
from jax.experimental import pallas as pl
from jax.experimental.pallas import tpu as pltpu
from jax.sharding import PartitionSpec as P

MESH = pl.DeviceIdType.MESH
LANES = 128
F32 = jnp.float32
BF16 = jnp.bfloat16


def iota(shape, axis):
    return lax.broadcasted_iota(jnp.int32, shape, axis)


def to_column(row):
    size = row.shape[1]
    eye = iota((size, size), 0) == iota((size, size), 1)
    return jnp.sum(jnp.where(eye, jnp.broadcast_to(row, (size, size)), 0.0), axis=1, keepdims=True)


def kernel(
    n,
    tp,
    page,
    state_hbm,
    gain_hbm,
    wqkv_hbm,
    wout_hbm,
    pool_hbm,
    len_hbm,
    table_hbm,
    dest_hbm,
    out_ref,
    state_ref,
    gain_ref,
    len_ref,
    table_ref,
    dest_ref,
    wqkv,
    wout,
    pool,
    outgoing,
    incoming,
    load_sem,
    move_send,
    move_recv,
):
    rows, width = state_ref.shape
    group = wout.shape[0] // LANES
    chunk = width // tp
    blocks = chunk // LANES
    tokens = pool.shape[0]
    page_count = tokens // page
    me = lax.axis_index("req")
    my_part = lax.axis_index("tp")

    steps = 4
    depth = width // steps
    loads = []
    for step in range(steps):
        span = pl.ds(step * depth, depth)
        loads.append(pltpu.make_async_copy(wqkv_hbm.at[span], wqkv.at[span], load_sem.at[step]))
    load_pool = pltpu.make_async_copy(pool_hbm, pool, load_sem.at[steps])
    load_wout = pltpu.make_async_copy(wout_hbm, wout, load_sem.at[steps + 1])
    small = []
    for slot, (src, dst) in enumerate(
        (
            (state_hbm, state_ref),
            (gain_hbm, gain_ref),
            (len_hbm, len_ref),
            (table_hbm, table_ref),
            (dest_hbm, dest_ref),
        )
    ):
        small.append(pltpu.make_async_copy(src, dst, load_sem.at[steps + 2 + slot]))
    for load in small + loads:
        load.start()
    load_pool.start()
    load_wout.start()

    barrier = pltpu.get_barrier_semaphore()

    def wrapped(value, size):
        return jnp.where(value >= size, value - size, value)

    def each_partner(act):
        def visit(shift, carry):
            peer = wrapped(me + shift, n)
            for part_shift in range(tp):
                if part_shift or not isinstance(shift, int) or shift:
                    act(peer, wrapped(my_part + part_shift, tp))
            return carry

        if n * tp <= 64:
            for shift in range(n):
                visit(shift, 0)
        else:
            for part_shift in range(1, tp):
                act(me, wrapped(my_part + part_shift, tp))
            lax.fori_loop(1, n, visit, 0)

    def greet(peer, part):
        pl.semaphore_signal(
            barrier, inc=1, device_id={"req": peer, "tp": part}, device_id_type=MESH
        )

    each_partner(greet)

    for load in small:
        load.wait()

    wide = state_ref[...].astype(F32)
    factor = lax.rsqrt(jnp.mean(wide * wide, axis=-1, keepdims=True) + 1e-05)
    normed = (wide * factor * gain_ref[...]).astype(BF16)

    length = to_column(len_ref[...].astype(F32))
    lane = iota((rows, LANES), 1)
    half = LANES // 2
    index = lax.rem(lane, half).astype(F32)
    freqs = jnp.exp(-math.log(1000000.0) * 2.0 * index / LANES)
    angles = length * freqs
    cosine = jnp.cos(angles)
    sine = jnp.sin(angles)
    sine = jnp.where(lane < half, -sine, sine)

    used = jnp.floor((length + (page - 1)) / page).astype(jnp.int32)
    table = table_ref[...]
    table = jnp.where(iota(table.shape, 1) < used, table, -1)
    padded = pl.cdiv(page_count, LANES) * LANES
    page_id = iota((rows, padded), 1)
    live_count = jnp.zeros((rows, padded), F32)
    for entry in range(table.shape[1]):
        left = length - float(entry * page)
        live_count = jnp.where(page_id == table[:, entry : entry + 1], left, live_count)
    live_count = jnp.clip(live_count, 0.0, float(page))
    per_block = LANES // page
    shifted = []
    for block in range(tokens // LANES):
        first = block * per_block
        base = first // LANES * LANES
        piece = live_count[:, base : base + LANES]
        if first != base:
            piece = pltpu.roll(piece, LANES - (first - base), 1)
        shifted.append(piece)
    spread = (iota((LANES, LANES), 0) == iota((LANES, LANES), 1) // page).astype(BF16)
    live_tokens = jnp.dot(
        jnp.concatenate(shifted, axis=0).astype(BF16), spread, preferred_element_type=F32
    )

    shift_bits = rows.bit_length() - 1
    target_row = lax.shift_right_logical(dest_ref[...], shift_bits).astype(F32)
    target = to_column(target_row)
    same = jnp.broadcast_to(target, (rows, rows)) == jnp.broadcast_to(target_row, (rows, rows))
    earlier = iota((rows, rows), 1) < iota((rows, rows), 0)
    rank = jnp.sum(jnp.where(same & earlier, 1.0, 0.0), axis=1, keepdims=True)
    source = (2 * me).astype(F32) - target
    source = jnp.where(source < 0, source + n, source)
    source = jnp.where(source >= n, source - n, source)
    key_out = (target * 2 + rank).astype(jnp.int32)
    key_in = (source * 2 + rank).astype(jnp.int32)
    flat = rows * blocks
    total_rows = n * 2 * blocks
    picked = iota((rows, flat), 0) == lax.rem(iota((rows, flat), 1), rows)
    key_row = jnp.sum(jnp.where(picked, key_out, 0).astype(F32), axis=0, keepdims=True).astype(
        jnp.int32
    )
    row_id = iota((total_rows, flat), 0)
    col_id = iota((total_rows, flat), 1)
    pack = (
        (row_id // blocks == key_row) & (lax.rem(row_id, blocks) == col_id // rows)
    ).astype(BF16)
    key_col = jnp.concatenate([key_in] * blocks, axis=0)
    row_id = iota((flat, total_rows), 0)
    col_id = iota((flat, total_rows), 1)
    unpack = (
        (col_id // blocks == key_col) & (lax.rem(col_id, blocks) == row_id // rows)
    ).astype(BF16)

    proj = None
    for step in range(steps):
        loads[step].wait()
        span = slice(step * depth, (step + 1) * depth)
        term = jnp.dot(normed[:, span], wqkv[span, :], preferred_element_type=F32)
        proj = term if proj is None else proj + term

    def rotated(values):
        return (values * cosine + pltpu.roll(values, half, 1) * sine).astype(BF16)

    heads = [rotated(proj[:, g * LANES : (g + 1) * LANES]) for g in range(group)]
    new_key = rotated(proj[:, group * LANES : (group + 1) * LANES])
    new_value = proj[:, (group + 1) * LANES :].astype(BF16)
    query = jnp.concatenate(heads, axis=0)

    scale = 1.0 / math.sqrt(LANES)
    load_pool.wait()
    scores = lax.dot_general(
        query, pool[:, :LANES], (((1,), (1,)), ((), ())), preferred_element_type=F32
    )
    offset = lax.rem(lane, page).astype(F32)
    masked = []
    for block in range(tokens // LANES):
        live = live_tokens[block * rows : (block + 1) * rows] > offset
        piece = scores[:, block * LANES : (block + 1) * LANES] * scale
        masked.append(
            jnp.concatenate(
                [
                    jnp.where(live, piece[g * rows : (g + 1) * rows], -jnp.inf)
                    for g in range(group)
                ],
                axis=0,
            )
        )
    scores = jnp.concatenate(masked, axis=1)
    keys = jnp.concatenate([new_key] * group, axis=0).astype(F32)
    values = jnp.concatenate([new_value] * group, axis=0).astype(F32)
    score_new = jnp.sum(query.astype(F32) * keys, axis=1, keepdims=True) * scale
    top = jnp.maximum(jnp.max(scores, axis=1, keepdims=True), score_new)
    weights = jnp.exp(scores - top)
    weight_new = jnp.exp(score_new - top)
    total = jnp.sum(weights, axis=1, keepdims=True) + weight_new
    numer = jnp.dot(weights.astype(BF16), pool[:, LANES:], preferred_element_type=F32)
    numer = numer + weight_new.astype(BF16).astype(F32) * values
    attn = (numer / total).astype(BF16)
    attn = jnp.concatenate([attn[g * rows : (g + 1) * rows] for g in range(group)], axis=1)

    load_wout.wait()
    term = jnp.dot(attn, wout[...], preferred_element_type=F32)
    mixed = (state_ref[...].astype(F32) * (1.0 / tp) + term).astype(BF16)

    piece_rows = 2 * blocks
    for part in range(tp):
        first = part * chunk
        stacked = jnp.concatenate(
            [mixed[:, first + b * LANES : first + (b + 1) * LANES] for b in range(blocks)], axis=0
        )
        packed = jnp.dot(pack, stacked, preferred_element_type=F32)
        outgoing[:, part * piece_rows : (part + 1) * piece_rows] = packed.reshape(
            n, piece_rows, LANES
        ).astype(BF16)
    pl.semaphore_wait(barrier, n * tp - 1)
    slot = my_part * n + me

    def send(peer, part):
        pltpu.make_async_remote_copy(
            src_ref=outgoing.at[peer],
            dst_ref=incoming.at[slot],
            send_sem=move_send,
            recv_sem=move_recv,
            device_id={"req": peer, "tp": part},
            device_id_type=MESH,
        ).start()

    each_partner(send)
    incoming[slot] = outgoing[me]
    all_but_one = incoming.at[pl.ds(0, n * tp - 1)]
    pltpu.make_async_copy(all_but_one, all_but_one, move_recv).wait()
    for part in range(tp):
        moved = None
        for origin in range(tp):
            received = incoming[
                origin * n : (origin + 1) * n, part * piece_rows : (part + 1) * piece_rows
            ].astype(F32)
            received = received.reshape(total_rows, LANES).astype(BF16)
            taken = jnp.dot(unpack, received, preferred_element_type=F32)
            moved = taken if moved is None else moved + taken
        moved = moved.astype(BF16)
        for b in range(blocks):
            first = part * chunk + b * LANES
            out_ref[:, first : first + LANES] = moved[b * rows : (b + 1) * rows]
    pltpu.make_async_copy(all_but_one, all_but_one, move_send).wait()


def local(n, tp, state, norm_gain, w_qkv, w_out, kv_cache, lengths, page_table, dest_slot):
    rows, width = state.shape
    page_count, _, page, entry = kv_cache.shape
    tokens = page_count * page
    chunk = width // tp
    blocks = chunk // LANES
    vmem = pl.BlockSpec(memory_space=pltpu.VMEM)
    hbm = pl.BlockSpec(memory_space=pltpu.HBM)
    return pl.pallas_call(
        functools.partial(kernel, n, tp, page),
        out_shape=pltpu.VMEM((rows, width), BF16),
        in_specs=[hbm] * 8,
        out_specs=vmem,
        scratch_shapes=[
            pltpu.VMEM((rows, width), BF16),
            pltpu.VMEM((1, width), F32),
            pltpu.VMEM((1, rows), jnp.int32),
            pltpu.VMEM(page_table.shape, jnp.int32),
            pltpu.VMEM((1, rows), jnp.int32),
            pltpu.VMEM((width, w_qkv.shape[2]), BF16),
            pltpu.VMEM((w_out.shape[1], width), BF16),
            pltpu.VMEM((tokens, entry), BF16),
            pltpu.VMEM((n, 2 * blocks * tp, LANES), BF16),
            pltpu.VMEM((n * tp, 2 * blocks * tp, LANES), BF16),
            pltpu.SemaphoreType.DMA((11,)),
            pltpu.SemaphoreType.DMA,
            pltpu.SemaphoreType.DMA,
        ],
        compiler_params=pltpu.CompilerParams(
            collective_id=0, has_side_effects=True, vmem_limit_bytes=60 * 1024 * 1024
        ),
    )(
        state,
        norm_gain.reshape(1, width),
        w_qkv.reshape(width, w_qkv.shape[2]),
        w_out[0],
        kv_cache.reshape(tokens, entry),
        lengths.reshape(1, rows),
        page_table,
        dest_slot.reshape(1, rows),
    )


def solution(mesh):
    placed = (
        P("req", None),
        P(),
        P(None, "tp", None),
        P("tp", None, None),
        P("req", "tp", None, None),
        P("req"),
        P("req", None),
        P("req"),
    )
    return jax.shard_map(
        functools.partial(local, mesh.shape["req"], mesh.shape["tp"]),
        mesh=mesh,
        in_specs=placed,
        out_specs=P("req", None),
        check_vma=False,
    )
```

```python
import functools
import math

import jax
import jax.numpy as jnp
from jax import lax
from jax.experimental import pallas as pl
from jax.experimental.pallas import tpu as pltpu
from jax.sharding import PartitionSpec as P

MESH = pl.DeviceIdType.MESH
LANES = 128
F32 = jnp.float32
BF16 = jnp.bfloat16


def iota(shape, axis):
    return lax.broadcasted_iota(jnp.int32, shape, axis)


def to_column(row):
    size = row.shape[1]
    eye = iota((size, size), 0) == iota((size, size), 1)
    return jnp.sum(jnp.where(eye, jnp.broadcast_to(row, (size, size)), 0.0), axis=1, keepdims=True)


def kernel(
    n,
    tp,
    page,
    state_hbm,
    gain_hbm,
    wqkv_hbm,
    wout_hbm,
    pool_hbm,
    len_hbm,
    table_hbm,
    dest_hbm,
    out_ref,
    state_ref,
    gain_ref,
    len_ref,
    table_ref,
    dest_ref,
    wqkv,
    wout,
    pool,
    parts,
    arrived,
    outgoing,
    incoming,
    load_sem,
    part_send,
    part_recv,
    move_send,
    move_recv,
):
    rows, width = state_ref.shape
    group = wout.shape[0] // LANES
    chunk = width // tp
    blocks = chunk // LANES
    tokens = pool.shape[0]
    page_count = tokens // page
    me = lax.axis_index("req")
    my_part = lax.axis_index("tp")

    steps = 4
    depth = width // steps
    loads = []
    for step in range(steps):
        span = pl.ds(step * depth, depth)
        loads.append(pltpu.make_async_copy(wqkv_hbm.at[span], wqkv.at[span], load_sem.at[step]))
    load_pool = pltpu.make_async_copy(pool_hbm, pool, load_sem.at[steps])
    load_wout = pltpu.make_async_copy(wout_hbm, wout, load_sem.at[steps + 1])
    small = []
    for slot, (src, dst) in enumerate(
        (
            (state_hbm, state_ref),
            (gain_hbm, gain_ref),
            (len_hbm, len_ref),
            (table_hbm, table_ref),
            (dest_hbm, dest_ref),
        )
    ):
        small.append(pltpu.make_async_copy(src, dst, load_sem.at[steps + 2 + slot]))
    for load in small + loads:
        load.start()
    load_pool.start()
    load_wout.start()

    barrier = pltpu.get_barrier_semaphore()

    def wrapped(value, size):
        return jnp.where(value >= size, value - size, value)

    def each_partner(act):
        def visit(shift, carry):
            peer = wrapped(me + shift, n)
            for part_shift in range(tp):
                if part_shift or not isinstance(shift, int) or shift:
                    act(peer, wrapped(my_part + part_shift, tp))
            return carry

        if n * tp <= 64:
            for shift in range(n):
                visit(shift, 0)
        else:
            for part_shift in range(1, tp):
                act(me, wrapped(my_part + part_shift, tp))
            lax.fori_loop(1, n, visit, 0)

    def greet(peer, part):
        pl.semaphore_signal(
            barrier, inc=1, device_id={"req": peer, "tp": part}, device_id_type=MESH
        )

    each_partner(greet)

    for load in small:
        load.wait()

    wide = state_ref[...].astype(F32)
    factor = lax.rsqrt(jnp.mean(wide * wide, axis=-1, keepdims=True) + 1e-05)
    normed = (wide * factor * gain_ref[...]).astype(BF16)

    length = to_column(len_ref[...].astype(F32))
    lane = iota((rows, LANES), 1)
    half = LANES // 2
    index = lax.rem(lane, half).astype(F32)
    freqs = jnp.exp(-math.log(1000000.0) * 2.0 * index / LANES)
    angles = length * freqs
    cosine = jnp.cos(angles)
    sine = jnp.sin(angles)
    sine = jnp.where(lane < half, -sine, sine)

    used = jnp.floor((length + (page - 1)) / page).astype(jnp.int32)
    table = table_ref[...]
    table = jnp.where(iota(table.shape, 1) < used, table, -1)
    padded = pl.cdiv(page_count, LANES) * LANES
    page_id = iota((rows, padded), 1)
    live_count = jnp.zeros((rows, padded), F32)
    for entry in range(table.shape[1]):
        left = length - float(entry * page)
        live_count = jnp.where(page_id == table[:, entry : entry + 1], left, live_count)
    live_count = jnp.clip(live_count, 0.0, float(page))
    per_block = LANES // page
    shifted = []
    for block in range(tokens // LANES):
        first = block * per_block
        base = first // LANES * LANES
        piece = live_count[:, base : base + LANES]
        if first != base:
            piece = pltpu.roll(piece, LANES - (first - base), 1)
        shifted.append(piece)
    spread = (iota((LANES, LANES), 0) == iota((LANES, LANES), 1) // page).astype(BF16)
    live_tokens = jnp.dot(
        jnp.concatenate(shifted, axis=0).astype(BF16), spread, preferred_element_type=F32
    )

    shift_bits = rows.bit_length() - 1
    target_row = lax.shift_right_logical(dest_ref[...], shift_bits).astype(F32)
    target = to_column(target_row)
    same = jnp.broadcast_to(target, (rows, rows)) == jnp.broadcast_to(target_row, (rows, rows))
    earlier = iota((rows, rows), 1) < iota((rows, rows), 0)
    rank = jnp.sum(jnp.where(same & earlier, 1.0, 0.0), axis=1, keepdims=True)
    source = (2 * me).astype(F32) - target
    source = jnp.where(source < 0, source + n, source)
    source = jnp.where(source >= n, source - n, source)
    key_out = (target * 2 + rank).astype(jnp.int32)
    key_in = (source * 2 + rank).astype(jnp.int32)
    flat = rows * blocks
    total_rows = n * 2 * blocks
    picked = iota((rows, flat), 0) == lax.rem(iota((rows, flat), 1), rows)
    key_row = jnp.sum(jnp.where(picked, key_out, 0).astype(F32), axis=0, keepdims=True).astype(
        jnp.int32
    )
    row_id = iota((total_rows, flat), 0)
    col_id = iota((total_rows, flat), 1)
    pack = (
        (row_id // blocks == key_row) & (lax.rem(row_id, blocks) == col_id // rows)
    ).astype(BF16)
    key_col = jnp.concatenate([key_in] * blocks, axis=0)
    row_id = iota((flat, total_rows), 0)
    col_id = iota((flat, total_rows), 1)
    unpack = (
        (col_id // blocks == key_col) & (lax.rem(col_id, blocks) == row_id // rows)
    ).astype(BF16)

    proj = None
    for step in range(steps):
        loads[step].wait()
        span = slice(step * depth, (step + 1) * depth)
        term = jnp.dot(normed[:, span], wqkv[span, :], preferred_element_type=F32)
        proj = term if proj is None else proj + term

    def rotated(values):
        return (values * cosine + pltpu.roll(values, half, 1) * sine).astype(BF16)

    heads = [rotated(proj[:, g * LANES : (g + 1) * LANES]) for g in range(group)]
    new_key = rotated(proj[:, group * LANES : (group + 1) * LANES])
    new_value = proj[:, (group + 1) * LANES :].astype(BF16)
    query = jnp.concatenate(heads, axis=0)

    scale = 1.0 / math.sqrt(LANES)
    load_pool.wait()
    scores = lax.dot_general(
        query, pool[:, :LANES], (((1,), (1,)), ((), ())), preferred_element_type=F32
    )
    offset = lax.rem(lane, page).astype(F32)
    masked = []
    for block in range(tokens // LANES):
        live = live_tokens[block * rows : (block + 1) * rows] > offset
        piece = scores[:, block * LANES : (block + 1) * LANES] * scale
        masked.append(
            jnp.concatenate(
                [
                    jnp.where(live, piece[g * rows : (g + 1) * rows], -jnp.inf)
                    for g in range(group)
                ],
                axis=0,
            )
        )
    scores = jnp.concatenate(masked, axis=1)
    keys = jnp.concatenate([new_key] * group, axis=0).astype(F32)
    values = jnp.concatenate([new_value] * group, axis=0).astype(F32)
    score_new = jnp.sum(query.astype(F32) * keys, axis=1, keepdims=True) * scale
    top = jnp.maximum(jnp.max(scores, axis=1, keepdims=True), score_new)
    weights = jnp.exp(scores - top)
    weight_new = jnp.exp(score_new - top)
    total = jnp.sum(weights, axis=1, keepdims=True) + weight_new
    numer = jnp.dot(weights.astype(BF16), pool[:, LANES:], preferred_element_type=F32)
    numer = numer + weight_new.astype(BF16).astype(F32) * values
    attn = (numer / total).astype(BF16)
    attn = jnp.concatenate([attn[g * rows : (g + 1) * rows] for g in range(group)], axis=1)

    load_wout.wait()
    pl.semaphore_wait(barrier, n * tp - 1)

    def columns(part):
        return pl.ds(pl.multiple_of(part * chunk, chunk), chunk)

    def part_copy(slot, landing, peer):
        return pltpu.make_async_remote_copy(
            src_ref=parts.at[slot],
            dst_ref=arrived.at[landing],
            send_sem=part_send.at[slot],
            recv_sem=part_recv.at[landing],
            device_id={"req": me, "tp": peer},
            device_id_type=MESH,
        )

    for shift in range(1, tp):
        peer = lax.rem(my_part + shift, tp)
        parts[peer] = jnp.dot(
            attn, wout[:, columns(peer)], preferred_element_type=F32
        ).astype(BF16)
        part_copy(peer, my_part, peer).start()
    summed = jnp.dot(attn, wout[:, columns(my_part)], preferred_element_type=F32)
    for shift in range(1, tp):
        peer = lax.rem(my_part + shift, tp)
        part_copy(peer, peer, peer).wait_recv()
        summed = summed + arrived[peer].astype(F32)
    mixed = (state_ref[:, columns(my_part)].astype(F32) + summed).astype(BF16)

    stacked = jnp.concatenate(
        [mixed[:, b * LANES : (b + 1) * LANES] for b in range(blocks)], axis=0
    )
    packed = jnp.dot(pack, stacked, preferred_element_type=F32)
    outgoing[...] = packed.reshape(n, 2 * blocks, LANES).astype(BF16)

    slot = my_part * n + me

    def send(peer, part):
        pltpu.make_async_remote_copy(
            src_ref=outgoing.at[peer],
            dst_ref=incoming.at[slot],
            send_sem=move_send,
            recv_sem=move_recv,
            device_id={"req": peer, "tp": part},
            device_id_type=MESH,
        ).start()

    each_partner(send)
    incoming[slot] = outgoing[me]
    all_but_one = incoming.at[pl.ds(0, n * tp - 1)]
    pltpu.make_async_copy(all_but_one, all_but_one, move_recv).wait()
    for part in range(tp):
        received = incoming[part * n : (part + 1) * n].astype(F32)
        received = received.reshape(total_rows, LANES).astype(BF16)
        moved = jnp.dot(unpack, received, preferred_element_type=F32).astype(BF16)
        for b in range(blocks):
            first = part * chunk + b * LANES
            out_ref[:, first : first + LANES] = moved[b * rows : (b + 1) * rows]
    for shift in range(1, tp):
        peer = lax.rem(my_part + shift, tp)
        part_copy(peer, my_part, peer).wait_send()
    pltpu.make_async_copy(all_but_one, all_but_one, move_send).wait()


def local(n, tp, state, norm_gain, w_qkv, w_out, kv_cache, lengths, page_table, dest_slot):
    rows, width = state.shape
    page_count, _, page, entry = kv_cache.shape
    tokens = page_count * page
    chunk = width // tp
    blocks = chunk // LANES
    vmem = pl.BlockSpec(memory_space=pltpu.VMEM)
    hbm = pl.BlockSpec(memory_space=pltpu.HBM)
    return pl.pallas_call(
        functools.partial(kernel, n, tp, page),
        out_shape=pltpu.VMEM((rows, width), BF16),
        in_specs=[hbm] * 8,
        out_specs=vmem,
        scratch_shapes=[
            pltpu.VMEM((rows, width), BF16),
            pltpu.VMEM((1, width), F32),
            pltpu.VMEM((1, rows), jnp.int32),
            pltpu.VMEM(page_table.shape, jnp.int32),
            pltpu.VMEM((1, rows), jnp.int32),
            pltpu.VMEM((width, w_qkv.shape[2]), BF16),
            pltpu.VMEM((w_out.shape[1], width), BF16),
            pltpu.VMEM((tokens, entry), BF16),
            pltpu.VMEM((tp, rows, chunk), BF16),
            pltpu.VMEM((tp, rows, chunk), BF16),
            pltpu.VMEM((n, 2 * blocks, LANES), BF16),
            pltpu.VMEM((n * tp, 2 * blocks, LANES), BF16),
            pltpu.SemaphoreType.DMA((11,)),
            pltpu.SemaphoreType.DMA((tp,)),
            pltpu.SemaphoreType.DMA((tp,)),
            pltpu.SemaphoreType.DMA,
            pltpu.SemaphoreType.DMA,
        ],
        compiler_params=pltpu.CompilerParams(
            collective_id=0, has_side_effects=True, vmem_limit_bytes=60 * 1024 * 1024
        ),
    )(
        state,
        norm_gain.reshape(1, width),
        w_qkv.reshape(width, w_qkv.shape[2]),
        w_out[0],
        kv_cache.reshape(tokens, entry),
        lengths.reshape(1, rows),
        page_table,
        dest_slot.reshape(1, rows),
    )


def solution(mesh):
    placed = (
        P("req", None),
        P(),
        P(None, "tp", None),
        P("tp", None, None),
        P("req", "tp", None, None),
        P("req"),
        P("req", None),
        P("req"),
    )
    return jax.shard_map(
        functools.partial(local, mesh.shape["req"], mesh.shape["tp"]),
        mesh=mesh,
        in_specs=placed,
        out_specs=P("req", None),
        check_vma=False,
    )
```
